32 devices in a mesh: users: 16 (over z, y, core), heads: 2 (over x).
Axes of the slice: x: 2, y: 2, z: 4, core: 2. Of those that a mesh axis runs over, the one named last changes fastest.
Arguments:
- sessions: bfloat16 [8192, 4096], P(('users', 'heads')), parts along dimension 0, may hold values from -16 to 16
- input_weight: bfloat16 [3, 4096, 2048], P(None, None, 'heads'), may hold values from -1 to 1
- output_weight: bfloat16 [2048, 4096], P('heads'), may hold values from -0.359375 to 0.359375
- session_counts: int32 [32], P('users'), parts along dimension 0, may hold values from 1 to 384, 512 in all
Outputs:
- attended: bfloat16 [8192, 4096], P(('users', 'heads')), parts along dimension 0
The draws below stay inside these ranges and needn't reach their ends.
There are 16 independent parts, one for each index of `users`. The reference program is written for one: setup_inputs(seed, part) draws one part's arguments, and reference() takes and returns one part's arrays. A program takes and returns all parts, laid end to end along the dimension named above; an argument that names none is the same for every part. Nothing has to cross between parts.
Inputs may be any that keep to these rules, and one draw needn't show every extreme that they name: `session_counts`: the 2 counts sum to 512.
All inputs are finite; a program needn't handle non-finite values.
Results may differ from the reference program's by a relative error of at most 0.015.
Values may be sent and summed in bfloat16 or wider, within the bound.
No kernel may reach another device: no remote copies, remote signals or barrier semaphores. Data moves between devices by JAX's collectives and lax.ppermute only.
A program may use at most 128 MiB of HBM per device.

```python
import math
import jax
import jax.numpy as jnp
import numpy as np
from jax import lax

D = 4096
HEADS = 16
HD = 128
HIST = 2
SESSIONS = 512
N_HEADS = 2


def draw_sessions(key, part):
    key_base = jax.random.fold_in(key, 0)
    result = jax.random.truncated_normal(key_base, -6.0, 6.0, (SESSIONS, D), jnp.float32)
    return result.astype(jnp.bfloat16)


def draw_input_weight(key, part):
    key_first, key_second, key_third = jax.random.split(key, 3)
    shape = (D, HEADS * HD)
    factor = D ** (-0.5)
    query_part = jax.random.truncated_normal(key_first, -6.0, 6.0, shape, jnp.float32) * factor
    key_part = jax.random.truncated_normal(key_second, -6.0, 6.0, shape, jnp.float32) * factor
    value_part = jax.random.truncated_normal(key_third, -6.0, 6.0, shape, jnp.float32) * factor
    return jnp.stack([query_part, key_part, value_part]).astype(jnp.bfloat16)


def steps_of(rng, extent, pieces, low, high):
    loudness, own = 1.0, jax.random.fold_in(rng, 6)
    for dim, parts in pieces:
        heights = jnp.exp(jax.random.uniform(jax.random.fold_in(own, dim), (parts,), jnp.float32, low / len(pieces), high / len(pieces)))
        loudness = loudness * jnp.repeat(heights, extent[dim] // parts).reshape([-1 if axis == dim else 1 for axis in range(len(extent))])
    return loudness


def profile(number_of, total, most, slope):
    weights = [(1 << 20) // math.isqrt(grade ** slope) + 1 for grade in range(2, number_of + 1)]
    spare, given = total - most - (number_of - 1), [1] * (number_of - 1)
    while spare > 0:
        free = [i for i in range(number_of - 1) if given[i] < most]
        pool, remaining = sum([weights[i] for i in free]), spare
        for i in free:
            addition = min(most - given[i], max(1, remaining * weights[i] // pool), spare)
            given[i] = given[i] + addition
            spare = spare - addition
    return np.array([most] + given)


def uneven_parts(stream_key, number_of, total, limit, lean):
    if number_of == 2:
        one = jax.random.randint(stream_key, (), max(1, total - limit), min(limit, total - 1) + 1)
        return jnp.stack([one, total - one])
    sizes = jnp.asarray(profile(number_of, total, limit, lean), jnp.int32)
    couples = (number_of - 1) // 2
    source_of, receiver = sizes[1:1 + 2 * couples:2], sizes[2:2 + 2 * couples:2]
    slack = jnp.minimum(source_of - 1, limit - receiver)
    passed = jax.random.randint(jax.random.fold_in(stream_key, 1), (couples,), 0, 1 << 20) % (slack + 1)
    sizes = sizes.at[1:1 + 2 * couples:2].set(source_of - passed).at[2:2 + 2 * couples:2].set(receiver + passed)
    return sizes[jax.random.permutation(jax.random.fold_in(stream_key, 2), number_of)]


def normal_values(rng, extent, spread, most, shards=(), held_as=jnp.bfloat16):
    factor_of = steps_of(rng, extent, shards, -0.22, 0.18) if shards else 1.0
    entries = jax.random.normal(rng, extent, jnp.float32) * spread * factor_of
    return jnp.minimum(jnp.maximum(entries, -most), most).astype(held_as)


def setup_inputs(seed: int = 0, part: int = 0) -> dict:
    key_list = jax.random.split(jax.random.key(seed), 5)
    part_splits = jax.random.split(jax.random.fold_in(key_list[4], part), 5)
    return {
        "sessions": draw_sessions(jax.random.fold_in(jax.random.fold_in(key_list[4], part), 71), part),
        "input_weight": draw_input_weight(jax.random.fold_in(key_list[4], 71), part),
        "output_weight": normal_values(key_list[2], (HEADS * HD, D), 0.06, 0.359375, ((0, 2),)),
        "session_counts": uneven_parts(part_splits[3], HIST, SESSIONS, SESSIONS * 3 // 4, 2).astype(jnp.int32),
    }


def permitted(total, counts):
    positions = jnp.arange(total, dtype=jnp.int32)
    ends = jnp.cumsum(counts).astype(jnp.int32)
    row_user = jnp.sum((positions[:, None] >= ends[None, :]).astype(jnp.int32), axis=1)
    same_user = row_user[:, None] == row_user[None, :]
    return jnp.logical_and(same_user, positions[:, None] >= positions[None, :])


def attend(packed, allowed):
    total = packed.shape[1]
    width = packed.shape[2]
    queries = packed[0].reshape(total, width // HD, HD).astype(jnp.float32)
    key_rows = packed[1].reshape(total, width // HD, HD).astype(jnp.float32)
    values = packed[2].reshape(total, width // HD, HD).astype(jnp.float32)
    scores = jnp.einsum("qhe,khe->hqk", queries, key_rows) * (HD ** -0.5)
    scores = jnp.where(allowed[None], scores, -1e30)
    highest = jnp.max(scores, axis=2, keepdims=True)
    raised = jnp.where(allowed[None], jnp.exp(scores - highest), 0.0)
    attn_probs = (raised / jnp.sum(raised, axis=2, keepdims=True)).astype(jnp.bfloat16)
    mixed = jnp.einsum("hqk,khe->qhe", attn_probs.astype(jnp.float32), values)
    return mixed.astype(jnp.bfloat16).reshape(total, width)


def reference(sessions, input_weight, output_weight, session_counts):
    total = sessions.shape[0]
    allowed = permitted(total, session_counts)
    packed = jnp.einsum("nd,cde->cne", sessions.astype(jnp.float32), input_weight.astype(jnp.float32)).astype(jnp.bfloat16)
    group_width = HEADS * HD // N_HEADS

    def one_group(running, index):
        begin = (index * group_width).astype(jnp.int32)
        part_cols = lax.dynamic_slice_in_dim(packed, begin, group_width, 2)
        mixed = attend(part_cols, allowed)
        weight_rows = lax.dynamic_slice_in_dim(output_weight, begin, group_width, 0)
        partial_value = jnp.dot(mixed, weight_rows, preferred_element_type=jnp.float32).astype(jnp.bfloat16)
        partial_value = lax.optimization_barrier(partial_value)
        return running + partial_value.astype(jnp.float32), None

    start_sum = jnp.zeros((total, sessions.shape[1]), jnp.float32)
    result, unused = lax.scan(one_group, start_sum, jnp.arange(N_HEADS, dtype=jnp.int32))
    return result.astype(jnp.bfloat16)
```

```python
import functools
import jax
import jax.numpy as jnp
import numpy as np
from jax import lax
from jax.experimental import pallas as pl
from jax.experimental.pallas import tpu as pltpu
from jax.sharding import PartitionSpec as P


HD = 128
PAIR = 2 * HD


def permitted(total, counts):
    positions = jnp.arange(total, dtype=jnp.int32)
    ends = jnp.cumsum(counts)
    row_user = jnp.sum((positions[:, None] >= ends[None, :]).astype(jnp.int32), axis=1)
    same_user = row_user[:, None] == row_user[None, :]
    return jnp.logical_and(same_user, positions[:, None] >= positions[None, :])


def attend(packed, allowed):
    total = packed.shape[1]
    width = packed.shape[2]
    block = min(512, total)
    count = total // block
    queries = packed[0].reshape(count, block, width // HD, HD)
    key_rows = packed[1].reshape(total, width // HD, HD)
    values = packed[2].reshape(total, width // HD, HD)
    masks = allowed.reshape(count, block, total)

    def one_block(pair):
        query_block, mask_block = pair
        scores = jnp.einsum(
            "qhe,khe->hqk", query_block, key_rows, preferred_element_type=jnp.float32
        ) * HD ** (-0.5)
        scores = jnp.where(mask_block[None], scores, -1e30)
        highest = jnp.max(scores, axis=2, keepdims=True)
        raised = jnp.where(mask_block[None], jnp.exp(scores - highest), 0.0)
        attn_probs = (raised / jnp.sum(raised, axis=2, keepdims=True)).astype(jnp.bfloat16)
        mixed = jnp.einsum("hqk,khe->qhe", attn_probs, values, preferred_element_type=jnp.float32)
        return mixed.astype(jnp.bfloat16).reshape(block, width)

    blocks_out = lax.map(one_block, (queries, masks))
    return blocks_out.reshape(total, width)


def gather_and_scatter(sessions, input_weight, output_weight, session_counts):
    packed = jnp.einsum(
        "nd,cde->cne",
        lax.all_gather(sessions, "heads", axis=0, tiled=True),
        input_weight,
        preferred_element_type=jnp.float32,
    ).astype(jnp.bfloat16)
    total = packed.shape[1]
    allowed = permitted(total, session_counts)
    mixed = attend(packed, allowed)
    return lax.psum_scatter(
        jnp.dot(mixed, output_weight, preferred_element_type=jnp.float32).astype(jnp.bfloat16),
        "heads",
        scatter_dimension=0,
        tiled=True,
    )


def chip_ring(mesh):
    column = mesh.devices.reshape(mesh.shape["users"], -1)[:, 0]
    by_chip = {}
    for user, device in enumerate(column):
        key = getattr(device, "coords", None)
        key = (user // 2,) if key is None else tuple(key)
        by_chip.setdefault(key, []).append(user)
    if any(len(users) != 2 for users in by_chip.values()):
        by_chip = {(i,): [2 * i, 2 * i + 1] for i in range(len(column) // 2)}
    keys = list(by_chip)

    def near(a, b):
        return sum(abs(i - j) for i, j in zip(a, b)) == 1

    budget = [20000]

    def extend(path, left):
        budget[0] -= 1
        if budget[0] < 0:
            return None
        if not left:
            return path if near(path[-1], path[0]) else None
        for key in sorted(k for k in left if near(k, path[-1])):
            found = extend(path + [key], left - {key})
            if found:
                return found
        return None

    order = extend([keys[0]], frozenset(keys[1:])) or keys
    return [tuple(by_chip[key]) for key in order]


def dot32(a, b):
    return jnp.dot(a, b, preferred_element_type=jnp.float32)


def scores_of(q, k):
    return lax.dot_general(q, k, (((1,), (1,)), ((), ())), preferred_element_type=jnp.float32)


def mask_of(counts_ref, query_base, key_base, rows):
    i = query_base + lax.broadcasted_iota(jnp.int32, (rows, 1), 0)
    first = jnp.zeros((rows, 1), jnp.int32)
    end = jnp.int32(0)
    for u in range(counts_ref.shape[0]):
        end = end + counts_ref[u]
        first = jnp.where(i >= end, end, first)
    j = key_base + lax.broadcasted_iota(jnp.int32, (rows, rows), 1)
    return jnp.logical_and(j <= i, j >= first)


def head_out(q, k_a, v_a, mask_a, k_b, v_b, mask_b):
    scale = HD ** (-0.5)
    s_a = jnp.where(mask_a, scores_of(q, k_a) * scale, -1e30)
    s_b = jnp.where(mask_b, scores_of(q, k_b) * scale, -1e30)
    top = jnp.maximum(jnp.max(s_a, axis=1, keepdims=True), jnp.max(s_b, axis=1, keepdims=True))
    p_a = jnp.exp(s_a - top)
    p_b = jnp.exp(s_b - top)
    total = jnp.sum(p_a, axis=1, keepdims=True) + jnp.sum(p_b, axis=1, keepdims=True)
    out = dot32(p_a.astype(jnp.bfloat16), v_a) + dot32(p_b.astype(jnp.bfloat16), v_b)
    return (out / total).astype(jnp.bfloat16)


def streamed(x, weight, kinds, offset, total, out_type):
    rows, depth = x.shape
    width = weight.shape[2]
    wide = min(2 * PAIR, width)
    across = width // wide
    n = len(kinds) * across
    first = kinds[0]

    def body(x_ref, w_hbm, *refs):
        o_ref, buf, sem = refs[-3:]

        def load(s):
            src = w_hbm.at[first + s // across, pl.ds(offset, depth), pl.ds(s % across * wide, wide)]
            return pltpu.make_async_copy(src, buf.at[s], sem.at[s])

        for s in range(n):
            load(s).start()

        @pl.loop(0, n)
        def _(s):
            pltpu.make_async_copy(
                w_hbm.at[0, pl.ds(0, depth), pl.ds(0, wide)], buf.at[s], sem.at[s]
            ).wait()
            at = pl.ds(pl.multiple_of(lax.rem(s, across) * wide, wide), wide)
            part = dot32(x_ref[...], buf[s])
            if total is not None:
                part = refs[0][s // across, :, at] + part
            o_ref[s // across, :, at] = part.astype(out_type)

    operands = (x, weight) if total is None else (x, weight, total)
    vmem = pl.BlockSpec(memory_space=pltpu.VMEM)
    return pl.pallas_call(
        body,
        in_specs=[vmem, pl.BlockSpec(memory_space=pl.ANY)] + [vmem] * (total is not None),
        out_specs=vmem,
        out_shape=jax.ShapeDtypeStruct((len(kinds), rows, width), out_type),
        scratch_shapes=[
            pltpu.VMEM((n, depth, wide), jnp.bfloat16),
            pltpu.SemaphoreType.DMA((n,)),
        ],
        cost_estimate=pl.CostEstimate(
            flops=2 * rows * depth * len(kinds) * width,
            bytes_accessed=2 * (rows * depth + len(kinds) * depth * width),
            transcendentals=0,
        ),
    )(*operands)


def finish_guests(place, counts, x, weight, offset, total, own, first_pair, pairs):
    rows, depth = x.shape
    kinds, _, _ = weight.shape
    step = offset // depth

    def body(place_ref, counts_ref, x_ref, w_ref, t_ref, own_ref, mixed_ref, kv_ref):
        mine = place_ref[0] * rows
        other = (1 - place_ref[0]) * rows
        mask_a = mask_of(counts_ref, other, mine, rows)
        mask_b = mask_of(counts_ref, other, other, rows)
        q, k, v = [
            (t_ref[c] + dot32(x_ref[...], w_ref[c])).astype(jnp.bfloat16) for c in range(3)
        ]
        kv_ref[0] = k
        kv_ref[1] = v
        for h in range(2):
            at = slice(h * HD, (h + 1) * HD)
            mixed_ref[:, at] = head_out(
                q[:, at], own_ref[0, :, at], own_ref[1, :, at], mask_a, k[:, at], v[:, at], mask_b
            )

    n = pairs
    return pl.pallas_call(
        body,
        grid_spec=pltpu.PrefetchScalarGridSpec(
            num_scalar_prefetch=2,
            grid=(n,),
            in_specs=[
                pl.BlockSpec((rows, depth), lambda p, *_: (0, 0)),
                pl.BlockSpec((kinds, depth, PAIR), lambda p, *_: (0, step, first_pair + p)),
                pl.BlockSpec((kinds, rows, PAIR), lambda p, *_: (0, 0, first_pair + p)),
                pl.BlockSpec((2, rows, PAIR), lambda p, *_: (0, 0, first_pair + p)),
            ],
            out_specs=[
                pl.BlockSpec((rows, PAIR), lambda p, *_: (0, p)),
                pl.BlockSpec((2, rows, PAIR), lambda p, *_: (0, 0, p)),
            ],
        ),
        out_shape=[
            jax.ShapeDtypeStruct((rows, n * PAIR), jnp.bfloat16),
            jax.ShapeDtypeStruct((2, rows, n * PAIR), jnp.bfloat16),
        ],
        cost_estimate=pl.CostEstimate(
            flops=2 * rows * depth * kinds * n * PAIR + 8 * rows * rows * n * PAIR,
            bytes_accessed=2 * kinds * depth * n * PAIR + 12 * kinds * rows * n * PAIR,
            transcendentals=4 * rows * rows * n,
        ),
    )(place, counts, x, weight, total, own)


def attend_own(place, counts, own_q, own_kv, kv, first_pair, pairs):
    rows = own_q.shape[1]

    def body(place_ref, counts_ref, q_ref, own_ref, kv_ref, mixed_ref):
        mine = place_ref[0] * rows
        other = (1 - place_ref[0]) * rows
        mask_a = mask_of(counts_ref, mine, mine, rows)
        mask_b = mask_of(counts_ref, mine, other, rows)
        for h in range(2):
            at = slice(h * HD, (h + 1) * HD)
            mixed_ref[:, at] = head_out(
                q_ref[0, :, at], own_ref[0, :, at], own_ref[1, :, at], mask_a,
                kv_ref[0, :, at], kv_ref[1, :, at], mask_b,
            )

    return pl.pallas_call(
        body,
        grid_spec=pltpu.PrefetchScalarGridSpec(
            num_scalar_prefetch=2,
            grid=(pairs,),
            in_specs=[
                pl.BlockSpec((1, rows, PAIR), lambda p, *_: (0, 0, first_pair + p)),
                pl.BlockSpec((2, rows, PAIR), lambda p, *_: (0, 0, first_pair + p)),
                pl.BlockSpec((2, rows, PAIR), lambda p, *_: (0, 0, p)),
            ],
            out_specs=pl.BlockSpec((rows, PAIR), lambda p, *_: (0, p)),
        ),
        out_shape=jax.ShapeDtypeStruct((rows, pairs * PAIR), jnp.bfloat16),
        cost_estimate=pl.CostEstimate(
            flops=8 * rows * rows * pairs * PAIR,
            bytes_accessed=12 * rows * pairs * PAIR,
            transcendentals=4 * rows * rows * pairs,
        ),
    )(place, counts, own_q, own_kv, kv)


def out_own(mixed_list, weight):
    rows = mixed_list[0].shape[0]
    depth, width = weight.shape
    wide = 4 * PAIR

    def body(*refs):
        w_ref, o_ref = refs[-2:]
        at, part = 0, None
        for ref in refs[:-2]:
            d = ref.shape[1]
            term = dot32(ref[...], w_ref[at:at + d, :])
            part = term if part is None else part + term
            at += d
        o_ref[...] = part

    return pl.pallas_call(
        body,
        grid=(width // wide,),
        in_specs=[pl.BlockSpec(m.shape, lambda n: (0, 0)) for m in mixed_list]
        + [pl.BlockSpec((depth, wide), lambda n: (0, n))],
        out_specs=pl.BlockSpec((rows, wide), lambda n: (0, n)),
        out_shape=jax.ShapeDtypeStruct((rows, width), jnp.float32),
        cost_estimate=pl.CostEstimate(
            flops=2 * rows * depth * width,
            bytes_accessed=2 * depth * width + 4 * rows * width,
            transcendentals=0,
        ),
    )(*mixed_list, weight)


def out_other(slots, mixed, row_offset, pieces, total, last):
    rows, depth = mixed.shape
    width = total.shape[1]
    wide = pieces[0].shape[-1]
    flat = []
    for i, array in enumerate(pieces):
        flat += [(i, s) for s in range(array.shape[0])]
    n = len(flat)
    out_type = jnp.bfloat16 if last else jnp.float32

    def body(slots_ref, mixed_ref, total_hbm, *refs):
        piece_refs, out_hbm = refs[:len(pieces)], refs[len(pieces)]
        w_buf, t_buf, o_buf, w_sem, t_sem, o_sem = refs[len(pieces) + 1:]

        def column(s):
            return pl.ds(pl.multiple_of(slots_ref[s] * wide, wide), wide)

        def loads(s):
            i, at = flat[s]
            src = piece_refs[i].at[at, pl.ds(row_offset, depth), :]
            return (
                pltpu.make_async_copy(src, w_buf.at[s], w_sem.at[s]),
                pltpu.make_async_copy(total_hbm.at[:, column(s)], t_buf.at[s], t_sem.at[s]),
            )

        def store(s):
            return pltpu.make_async_copy(o_buf.at[s], out_hbm.at[:, column(s)], o_sem.at[s])

        for s in range(n):
            for copy in loads(s):
                copy.start()
        for s in range(n):
            for copy in loads(s):
                copy.wait()
            o_buf[s] = (t_buf[s] + dot32(mixed_ref[...], w_buf[s])).astype(out_type)
            store(s).start()
        for s in range(n):
            store(s).wait()

    return pl.pallas_call(
        body,
        grid_spec=pltpu.PrefetchScalarGridSpec(
            num_scalar_prefetch=1,
            grid=(1,),
            in_specs=[
                pl.BlockSpec(mixed.shape, lambda i, *_: (0, 0)),
                pl.BlockSpec(memory_space=pl.ANY),
            ]
            + [pl.BlockSpec(memory_space=pl.ANY)] * len(pieces),
            out_specs=pl.BlockSpec(memory_space=pl.ANY),
            scratch_shapes=[
                pltpu.VMEM((n, depth, wide), jnp.bfloat16),
                pltpu.VMEM((n, rows, wide), jnp.float32),
                pltpu.VMEM((n, rows, wide), out_type),
                pltpu.SemaphoreType.DMA((n,)),
                pltpu.SemaphoreType.DMA((n,)),
                pltpu.SemaphoreType.DMA((n,)),
            ],
        ),
        out_shape=jax.ShapeDtypeStruct((rows, width), out_type),
        cost_estimate=pl.CostEstimate(
            flops=2 * rows * depth * width,
            bytes_accessed=2 * depth * width + 6 * rows * width,
            transcendentals=0,
        ),
    )(slots, mixed, total, *pieces)


def two_halves(ring, sessions, input_weight, output_weight, session_counts):
    users = 2 * len(ring)
    chips = len(ring)
    _, model = sessions.shape
    width = input_weight.shape[2]
    pairs = width // PAIR
    place = lax.axis_index("heads").astype(jnp.int32)[None]
    user = lax.axis_index("users")

    across = [(0, 1), (1, 0)]
    beside = [(a, b) for pair in ring for a, b in (pair, pair[::-1])]
    around = []
    for i in range(chips):
        around.append((ring[i][0], ring[(i + 1) % chips][0]))
        around.append((ring[i][1], ring[(i - 1) % chips][1]))

    full = (chips - 1) // 2
    half = chips % 2 == 0
    table = np.zeros((users, users), np.int32)
    for i in range(chips):
        for core in range(2):
            held = [(i, core), (i, 1 - core)]
            for k in range(1, full + 1):
                for c in (core, 1 - core):
                    source = (i - k) % chips if c == 0 else (i + k) % chips
                    held += [(source, c), (source, 1 - c)]
            if half:
                far = (i + chips // 2) % chips
                held += [(far, core), (far, 1 - core)]
            table[ring[i][core]] = [2 * a + b for a, b in held]
    slots = jnp.asarray(table)[user]
    piece_width = model // users
    start = slots[0] * piece_width
    piece = lax.dynamic_slice_in_dim(output_weight, start, piece_width, 1)

    crossed = lax.ppermute(piece, "heads", across)
    sizes = [model // 2, model // 4, model // 8, model // 8]
    offsets = np.cumsum([0] + sizes)[:-1].tolist()
    guests = [lax.ppermute(sessions[:, o:o + s], "heads", across) for o, s in zip(offsets, sizes)]

    partner = lax.ppermute(crossed, "users", beside)
    stack = jnp.stack([crossed, partner])
    pieces = [stack]
    moving = stack
    for _ in range(full):
        moving = lax.ppermute(moving, "users", around)
        pieces += [moving, lax.ppermute(moving, "users", beside)]
    if half:
        far = lax.ppermute(moving[:1], "users", around)
        pieces += [far, lax.ppermute(far, "users", beside)]

    own_q = streamed(sessions, input_weight, (0,), 0, None, jnp.bfloat16)
    own_kv = streamed(sessions, input_weight, (1, 2), 0, None, jnp.bfloat16)
    total = None
    for i in range(len(sizes) - 1):
        total = streamed(
            guests[i], input_weight, (0, 1, 2), offsets[i], total,
            jnp.float32,
        )
    groups = [(0, pairs // 2), (pairs // 2, pairs - pairs // 2)]
    groups = [g for g in groups if g[1]]
    mixed_far, mixed_own = [], []
    for first, n in groups:
        mixed, kv = finish_guests(
            place, session_counts, guests[-1], input_weight,
            offsets[-1], total, own_kv, first, n,
        )
        mixed_far.append(lax.ppermute(mixed, "heads", across))
        mixed_own.append(attend_own(place, session_counts, own_q, own_kv, kv, first, n))
    out = out_own(mixed_own, output_weight)
    for i, (first, n) in enumerate(groups):
        out = out_other(
            slots, mixed_far[i], first * PAIR, pieces, out,
            i == len(groups) - 1,
        )
    return out


def solution(mesh):
    in_specs = (P(("users", "heads"), None), P(None, None, "heads"), P("heads", None), P("users"))
    out_specs = P(("users", "heads"), None)
    if mesh.shape["heads"] == 2 and mesh.shape["users"] % 2 == 0 and mesh.shape["users"] > 2:
        per_device = functools.partial(two_halves, chip_ring(mesh))

        def layer(*args):
            return per_device(*args)

        return jax.shard_map(
            layer, mesh=mesh, in_specs=in_specs, out_specs=out_specs, check_vma=False
        )
    return jax.shard_map(
        gather_and_scatter, mesh=mesh, in_specs=in_specs, out_specs=out_specs, check_vma=False
    )
```

```python
import functools
import jax
import jax.numpy as jnp
import numpy as np
from jax import lax
from jax.experimental import pallas as pl
from jax.experimental.pallas import tpu as pltpu
from jax.sharding import PartitionSpec as P


HD = 128


def permitted(total, counts):
    positions = jnp.arange(total, dtype=jnp.int32)
    ends = jnp.cumsum(counts)
    row_user = jnp.sum((positions[:, None] >= ends[None, :]).astype(jnp.int32), axis=1)
    same_user = row_user[:, None] == row_user[None, :]
    return jnp.logical_and(same_user, positions[:, None] >= positions[None, :])


def attend(packed, allowed):
    total = packed.shape[1]
    width = packed.shape[2]
    block = min(512, total)
    count = total // block
    queries = packed[0].reshape(count, block, width // HD, HD)
    key_rows = packed[1].reshape(total, width // HD, HD)
    values = packed[2].reshape(total, width // HD, HD)
    masks = allowed.reshape(count, block, total)

    def one_block(pair):
        query_block, mask_block = pair
        scores = jnp.einsum(
            "qhe,khe->hqk", query_block, key_rows, preferred_element_type=jnp.float32
        ) * HD ** (-0.5)
        scores = jnp.where(mask_block[None], scores, -1e30)
        highest = jnp.max(scores, axis=2, keepdims=True)
        raised = jnp.where(mask_block[None], jnp.exp(scores - highest), 0.0)
        attn_probs = (raised / jnp.sum(raised, axis=2, keepdims=True)).astype(jnp.bfloat16)
        mixed = jnp.einsum("hqk,khe->qhe", attn_probs, values, preferred_element_type=jnp.float32)
        return mixed.astype(jnp.bfloat16).reshape(block, width)

    blocks_out = lax.map(one_block, (queries, masks))
    return blocks_out.reshape(total, width)


def gather_and_scatter(sessions, input_weight, output_weight, session_counts):
    packed = jnp.einsum(
        "nd,cde->cne",
        lax.all_gather(sessions, "heads", axis=0, tiled=True),
        input_weight,
        preferred_element_type=jnp.float32,
    ).astype(jnp.bfloat16)
    total = packed.shape[1]
    allowed = permitted(total, session_counts)
    mixed = attend(packed, allowed)
    return lax.psum_scatter(
        jnp.dot(mixed, output_weight, preferred_element_type=jnp.float32).astype(jnp.bfloat16),
        "heads",
        scatter_dimension=0,
        tiled=True,
    )


def chip_ring(mesh):
    column = mesh.devices.reshape(mesh.shape["users"], -1)[:, 0]
    by_chip = {}
    for user, device in enumerate(column):
        key = getattr(device, "coords", None)
        key = (user // 2,) if key is None else tuple(key)
        by_chip.setdefault(key, []).append(user)
    if any(len(users) != 2 for users in by_chip.values()):
        by_chip = {(i,): [2 * i, 2 * i + 1] for i in range(len(column) // 2)}
    keys = list(by_chip)

    def near(a, b):
        return sum(abs(i - j) for i, j in zip(a, b)) == 1

    budget = [20000]

    def extend(path, left):
        budget[0] -= 1
        if budget[0] < 0:
            return None
        if not left:
            return path if near(path[-1], path[0]) else None
        for key in sorted(k for k in left if near(k, path[-1])):
            found = extend(path + [key], left - {key})
            if found:
                return found
        return None

    order = extend([keys[0]], frozenset(keys[1:])) or keys
    return [tuple(by_chip[key]) for key in order]


def dot32(a, b):
    return jnp.dot(a, b, preferred_element_type=jnp.float32)


def scores_of(q, k):
    return lax.dot_general(q, k, (((1,), (1,)), ((), ())), preferred_element_type=jnp.float32)


LOG2E = 1.4426950408889634
VMEM = pl.BlockSpec(memory_space=pltpu.VMEM)
SMEM = pl.BlockSpec(memory_space=pltpu.SMEM)
HBM = pl.BlockSpec(memory_space=pltpu.HBM)


def call(
    body, in_specs, out_shape, operands, flops, scratch=(), aliases=None, out_specs=None, mib=8
):
    spaces = {id(VMEM): pltpu.VMEM, id(HBM): pltpu.HBM}
    operands = [
        pltpu.with_memory_space_constraint(x, spaces[id(spec)]) if id(spec) in spaces else x
        for spec, x in zip(in_specs, operands)
    ]
    return pl.pallas_call(
        body,
        in_specs=in_specs,
        out_specs=out_specs if out_specs is not None else jax.tree.map(lambda _: VMEM, out_shape),
        out_shape=out_shape,
        scratch_shapes=list(scratch),
        input_output_aliases=aliases or {},
        compiler_params=pltpu.CompilerParams(vmem_limit_bytes=mib << 20),
        cost_estimate=pl.CostEstimate(flops=flops, bytes_accessed=1 << 20, transcendentals=0),
    )(*operands)


def load_piece(user, place, output_weight, piece_width):
    depth = output_weight.shape[0]

    def body(user_ref, place_ref, w_hbm, o_ref, sem):
        at = pl.ds(pl.multiple_of(user_ref[0] * piece_width, piece_width), piece_width)
        copy = pltpu.make_async_copy(w_hbm.at[:, at], o_ref, sem)
        copy.start()
        copy.wait()

    return call(
        body, [SMEM, SMEM, HBM], pltpu.VMEM((depth, piece_width), jnp.bfloat16),
        (user, place, output_weight), 0, [pltpu.SemaphoreType.DMA(())],
    )


def load_rows(sessions, sizes):
    rows = sessions.shape[0]
    offsets = np.cumsum([0] + sizes)[:-1].tolist()
    n = len(sizes)

    def body(x_hbm, *refs):
        outs, sem = refs[:-1], refs[-1]
        copies = []
        for i in range(n):
            src = x_hbm.at[:, pl.ds(offsets[i], sizes[i])]
            copies.append(pltpu.make_async_copy(src, outs[i], sem.at[i]))
        for copy in copies:
            copy.start()
        for copy in copies:
            copy.wait()

    return call(
        body, [HBM], [pltpu.VMEM((rows, s), jnp.bfloat16) for s in sizes],
        (sessions,), 0, [pltpu.SemaphoreType.DMA((n,))],
    )


def project(parts, weight, kinds, wide):
    rows = parts[0].shape[0]
    _, depth, width = weight.shape
    across = width // wide
    n = len(kinds) * across
    first = kinds[0]

    def body(*refs):
        x_refs, (w_hbm, o_ref, buf, sem) = refs[:len(parts)], refs[len(parts):]

        def load(s):
            src = w_hbm.at[first + s // across, :, pl.ds(s % across * wide, wide)]
            return pltpu.make_async_copy(src, buf.at[s], sem.at[s])

        for s in range(n):
            load(s).start()

        @pl.loop(0, n)
        def _(s):
            pltpu.make_async_copy(w_hbm.at[0, :, pl.ds(0, wide)], buf.at[s], sem.at[s]).wait()
            at, total = 0, None
            for x_ref in x_refs:
                d = x_ref.shape[1]
                term = dot32(x_ref[...], buf[s, at:at + d, :])
                total = term if total is None else total + term
                at += d
            cols = pl.ds(pl.multiple_of(lax.rem(s, across) * wide, wide), wide)
            o_ref[s // across, :, cols] = total.astype(jnp.bfloat16)

    return call(
        body, [VMEM] * len(parts) + [HBM],
        [
            pltpu.VMEM((len(kinds), rows, width), jnp.bfloat16),
            pltpu.VMEM((n, depth, wide), jnp.bfloat16),
        ],
        (*parts, weight), 2 * rows * depth * len(kinds) * width,
        [pltpu.SemaphoreType.DMA((n,))],
    )


def project_part(x, weights, offset, total):
    rows, depth = x.shape
    blocks = sum(w.shape[0] for w in weights)
    wide = weights[0].shape[2]
    across = blocks // 3

    def body(x_ref, *refs):
        w_refs, o_ref = refs[:len(weights)], refs[-1]
        base = 0
        for w_ref in w_refs:
            n = w_ref.shape[0]

            @pl.loop(0, n)
            def _(s, w_ref=w_ref, base=base):
                t = s + base
                at = pl.ds(pl.multiple_of(lax.rem(t, across) * wide, wide), wide)
                part = dot32(x_ref[...], w_ref[s, offset:offset + depth, :])
                if total is not None:
                    part = refs[len(weights)][t // across, :, at] + part
                o_ref[t // across, :, at] = part

            base += n

    operands = (x, *weights) + (() if total is None else (total,))
    return call(
        body, [VMEM] * len(operands),
        pltpu.VMEM((3, rows, across * wide), jnp.float32), operands,
        2 * rows * depth * blocks * wide,
        aliases={} if total is None else {len(operands) - 1: 0},
    )


def biases(place, counts, rows):
    def body(place_ref, counts_ref, o_ref):
        mine = place_ref[0] * rows
        other = (1 - place_ref[0]) * rows
        for n, (query, key) in enumerate(((mine, mine), (mine, other), (other, mine), (other, other))):
            i = query + lax.broadcasted_iota(jnp.int32, (rows, 1), 0)
            first = jnp.zeros((rows, 1), jnp.int32)
            end = jnp.int32(0)
            for u in range(counts_ref.shape[0]):
                end = end + counts_ref[u]
                first = jnp.where(i >= end, end, first)
            j = key + lax.broadcasted_iota(jnp.int32, (rows, rows), 1)
            allowed = jnp.logical_and(j <= i, j >= first)
            o_ref[n] = jnp.where(allowed, 0.0, -1e30)

    return call(body, [SMEM, SMEM], pltpu.VMEM((4, rows, rows), jnp.float32), (place, counts), 0)


def head_out(q, keys, values, masks):
    scores = [scores_of(q, k) * (HD ** (-0.5) * LOG2E) + b for k, b in zip(keys, masks)]
    top = functools.reduce(jnp.maximum, [jnp.max(s, axis=1, keepdims=True) for s in scores])
    raised = [jnp.exp2(s - top) for s in scores]
    total = sum(jnp.sum(p, axis=1, keepdims=True) for p in raised)
    out = sum(dot32(p.astype(jnp.bfloat16), v) for p, v in zip(raised, values))
    return (out / total).astype(jnp.bfloat16)


def finish(x, weights, offset, total, own_k, own_v, bias, g):
    rows, depth = x.shape
    wide = weights[0].shape[2]
    across = total.shape[2] // wide
    cols = slice(g * wide, (g + 1) * wide)
    where = [(i, s) for i, w in enumerate(weights) for s in range(w.shape[0])]

    def body(x_ref, *refs):
        w_refs = refs[:len(weights)]
        t_ref, k_ref, v_ref, bias_ref, mixed_ref, kv_ref = refs[len(weights):]
        packed = []
        for c in range(3):
            i, s = where[c * across + g]
            part = dot32(x_ref[...], w_refs[i][s, offset:offset + depth, :])
            packed.append((t_ref[c, :, cols] + part).astype(jnp.bfloat16))
        q, k, v = packed
        kv_ref[0] = k
        kv_ref[1] = v
        for h in range(wide // HD):
            at = slice(h * HD, (h + 1) * HD)
            there = slice(g * wide + h * HD, g * wide + (h + 1) * HD)
            mixed_ref[:, at] = head_out(
                q[:, at], (k[:, at], k_ref[0, :, there]), (v[:, at], v_ref[0, :, there]),
                (bias_ref[3], bias_ref[2]),
            )

    operands = (x, *weights, total, own_k, own_v, bias)
    return call(
        body, [VMEM] * len(operands),
        [pltpu.VMEM((rows, wide), jnp.bfloat16), pltpu.VMEM((2, rows, wide), jnp.bfloat16)],
        operands, 6 * rows * depth * wide + 8 * rows * rows * wide,
    )


def own_out(own_q, own_k, own_v, kvs, bias, weight):
    _, rows, width = own_q.shape
    model = weight.shape[1]
    wide = kvs[0].shape[2]
    step = min(512, model)
    n = model // step

    def body(q_ref, k_ref, v_ref, *refs):
        kv_refs = refs[:len(kvs)]
        bias_ref, w_hbm, o_ref, buf, mixed, sem = refs[len(kvs):]

        def load(s):
            return pltpu.make_async_copy(w_hbm.at[:, pl.ds(s * step, step)], buf.at[s], sem.at[s])

        for s in range(n):
            load(s).start()
        for h in range(width // HD):
            at = slice(h * HD, (h + 1) * HD)
            kv_ref, here = kv_refs[h * HD // wide], slice(h * HD % wide, h * HD % wide + HD)
            mixed[:, at] = head_out(
                q_ref[0, :, at], (k_ref[0, :, at], kv_ref[0, :, here]),
                (v_ref[0, :, at], kv_ref[1, :, here]), (bias_ref[0], bias_ref[1]),
            )

        @pl.loop(0, n)
        def _(s):
            pltpu.make_async_copy(w_hbm.at[:, pl.ds(0, step)], buf.at[s], sem.at[s]).wait()
            cols = pl.ds(pl.multiple_of(s * step, step), step)
            o_ref[:, cols] = dot32(mixed[...], buf[s])

    return call(
        body, [VMEM] * (3 + len(kvs)) + [VMEM, HBM],
        pltpu.VMEM((rows, model), jnp.float32), (own_q, own_k, own_v, *kvs, bias, weight),
        2 * rows * width * model + 8 * rows * rows * width,
        [
            pltpu.VMEM((n, width, step), jnp.bfloat16),
            pltpu.VMEM((rows, width), jnp.bfloat16),
            pltpu.SemaphoreType.DMA((n,)),
        ],
        mib=6 + (2 * width * model >> 20),
    )


def other_out(user, table, mixed, row_offset, pieces, total, last):
    rows, depth = mixed.shape
    model = total.shape[1]
    wide = pieces[0].shape[-1]
    n = len(pieces)

    def body(user_ref, table_ref, mixed_ref, total_ref, *refs):
        piece_refs, o_ref = refs[:len(pieces)], refs[len(pieces)]

        def columns(s):
            return pl.ds(pl.multiple_of(table_ref[user_ref[0] * n + s] * wide, wide), wide)

        if last:
            buf, sem = refs[len(pieces) + 1:]

            def store(s):
                return pltpu.make_async_copy(buf.at[s], o_ref.at[:, columns(s)], sem.at[s])

        for s in range(n):
            part = dot32(mixed_ref[...], piece_refs[s][row_offset:row_offset + depth, :])
            part = total_ref[:, columns(s)] + part
            if last:
                buf[s] = part.astype(jnp.bfloat16)
                store(s).start()
            else:
                o_ref[:, columns(s)] = part
        if last:
            for s in range(n):
                store(s).wait()

    operands = (user, table, mixed, total, *pieces)
    return call(
        body, [SMEM, SMEM] + [VMEM] * (2 + len(pieces)),
        jax.ShapeDtypeStruct((rows, model), jnp.bfloat16) if last else pltpu.VMEM((rows, model), jnp.float32),
        operands, 2 * rows * depth * model,
        [pltpu.VMEM((n, rows, wide), jnp.bfloat16), pltpu.SemaphoreType.DMA((n,))] if last else (),
        aliases={} if last else {3: 0},
        out_specs=HBM if last else VMEM,
    )


def two_halves(ring, sessions, input_weight, output_weight, session_counts):
    users = 2 * len(ring)
    chips = len(ring)
    rows, model = sessions.shape
    width = input_weight.shape[2]
    wide = min(512, width)
    place = lax.axis_index("heads").astype(jnp.int32)[None]
    user = lax.axis_index("users").astype(jnp.int32)[None]

    across = [(0, 1), (1, 0)]
    beside = [(a, b) for pair in ring for a, b in (pair, pair[::-1])]
    around = []
    for i in range(chips):
        around.append((ring[i][0], ring[(i + 1) % chips][0]))
        around.append((ring[i][1], ring[(i - 1) % chips][1]))

    full = (chips - 1) // 2
    half = chips % 2 == 0
    table = np.zeros((users, users), np.int32)
    for i in range(chips):
        for core in range(2):
            held = [(i, core), (i, 1 - core)]
            for k in range(1, full + 1):
                for c in (core, 1 - core):
                    source = (i - k) % chips if c == 0 else (i + k) % chips
                    held += [(source, c), (source, 1 - c)]
            if half:
                far = (i + chips // 2) % chips
                held += [(far, core), (far, 1 - core)]
            table[ring[i][core]] = [ring[a][b] for a, b in held]
    table = jnp.asarray(table.reshape(-1))

    sizes = [model // 2, model // 4, model // 8, model // 8]
    offsets = np.cumsum([0] + sizes)[:-1].tolist()
    piece = load_piece(user, place, output_weight, model // users)
    parts = load_rows(sessions, sizes)

    crossed = lax.ppermute(piece, "heads", across)
    guests = [lax.ppermute(x, "heads", across) for x in parts]

    near, far = crossed, lax.ppermute(crossed, "users", beside)
    pieces = [near, far]
    for _ in range(full):
        near = lax.ppermute(near, "users", around)
        far = lax.ppermute(far, "users", around)
        pieces += [near, far]
        pieces += [lax.ppermute(near, "users", beside), lax.ppermute(far, "users", beside)]
    if half:
        near = lax.ppermute(near, "users", around)
        pieces += [near, lax.ppermute(near, "users", beside)]

    own_q, w_q = project(parts, input_weight, (0,), wide)
    own_k, w_k = project(parts, input_weight, (1,), wide)
    own_v, w_v = project(parts, input_weight, (2,), wide)
    weights = (w_q, w_k, w_v)
    bias = biases(place, session_counts, rows)
    total = None
    for i in range(len(sizes) - 1):
        total = project_part(guests[i], weights, offsets[i], total)
    mixed_far, kvs = [], []
    for g in range(width // wide):
        mixed, kv = finish(guests[-1], weights, offsets[-1], total, own_k, own_v, bias, g)
        mixed_far.append(lax.ppermute(mixed, "heads", across))
        kvs.append(kv)
    out = own_out(own_q, own_k, own_v, kvs, bias, output_weight)
    for g, mixed in enumerate(mixed_far):
        out = other_out(user, table, mixed, g * wide, pieces, out, g == len(mixed_far) - 1)
    return out


def solution(mesh):
    in_specs = (P(("users", "heads"), None), P(None, None, "heads"), P("heads", None), P("users"))
    out_specs = P(("users", "heads"), None)
    if mesh.shape["heads"] == 2 and mesh.shape["users"] % 2 == 0 and mesh.shape["users"] > 2:
        per_device = functools.partial(two_halves, chip_ring(mesh))

        def layer(*args):
            return per_device(*args)

        return jax.shard_map(
            layer, mesh=mesh, in_specs=in_specs, out_specs=out_specs, check_vma=False
        )
    return jax.shard_map(
        gather_and_scatter, mesh=mesh, in_specs=in_specs, out_specs=out_specs, check_vma=False
    )
```

```python
import functools
import jax
import jax.numpy as jnp
import numpy as np
from jax import lax
from jax.experimental import pallas as pl
from jax.experimental.pallas import tpu as pltpu
from jax.sharding import PartitionSpec as P


HD = 128


def permitted(total, counts):
    positions = jnp.arange(total, dtype=jnp.int32)
    ends = jnp.cumsum(counts)
    row_user = jnp.sum((positions[:, None] >= ends[None, :]).astype(jnp.int32), axis=1)
    same_user = row_user[:, None] == row_user[None, :]
    return jnp.logical_and(same_user, positions[:, None] >= positions[None, :])


def attend(packed, allowed):
    total = packed.shape[1]
    width = packed.shape[2]
    block = min(512, total)
    count = total // block
    queries = packed[0].reshape(count, block, width // HD, HD)
    key_rows = packed[1].reshape(total, width // HD, HD)
    values = packed[2].reshape(total, width // HD, HD)
    masks = allowed.reshape(count, block, total)

    def one_block(pair):
        query_block, mask_block = pair
        scores = jnp.einsum(
            "qhe,khe->hqk", query_block, key_rows, preferred_element_type=jnp.float32
        ) * HD ** (-0.5)
        scores = jnp.where(mask_block[None], scores, -1e30)
        highest = jnp.max(scores, axis=2, keepdims=True)
        raised = jnp.where(mask_block[None], jnp.exp(scores - highest), 0.0)
        attn_probs = (raised / jnp.sum(raised, axis=2, keepdims=True)).astype(jnp.bfloat16)
        mixed = jnp.einsum("hqk,khe->qhe", attn_probs, values, preferred_element_type=jnp.float32)
        return mixed.astype(jnp.bfloat16).reshape(block, width)

    blocks_out = lax.map(one_block, (queries, masks))
    return blocks_out.reshape(total, width)


def gather_and_scatter(sessions, input_weight, output_weight, session_counts):
    packed = jnp.einsum(
        "nd,cde->cne",
        lax.all_gather(sessions, "heads", axis=0, tiled=True),
        input_weight,
        preferred_element_type=jnp.float32,
    ).astype(jnp.bfloat16)
    total = packed.shape[1]
    allowed = permitted(total, session_counts)
    mixed = attend(packed, allowed)
    return lax.psum_scatter(
        jnp.dot(mixed, output_weight, preferred_element_type=jnp.float32).astype(jnp.bfloat16),
        "heads",
        scatter_dimension=0,
        tiled=True,
    )


def chip_ring(mesh):
    column = mesh.devices.reshape(mesh.shape["users"], -1)[:, 0]
    by_chip = {}
    for user, device in enumerate(column):
        key = getattr(device, "coords", None)
        key = (user // 2,) if key is None else tuple(key)
        by_chip.setdefault(key, []).append(user)
    if any(len(users) != 2 for users in by_chip.values()):
        by_chip = {(i,): [2 * i, 2 * i + 1] for i in range(len(column) // 2)}
    keys = list(by_chip)

    def near(a, b):
        return sum(abs(i - j) for i, j in zip(a, b)) == 1

    budget = [20000]

    def extend(path, left):
        budget[0] -= 1
        if budget[0] < 0:
            return None
        if not left:
            return path if near(path[-1], path[0]) else None
        for key in sorted(k for k in left if near(k, path[-1])):
            found = extend(path + [key], left - {key})
            if found:
                return found
        return None

    order = extend([keys[0]], frozenset(keys[1:])) or keys
    return [tuple(by_chip[key]) for key in order]


def dot32(a, b):
    return jnp.dot(a, b, preferred_element_type=jnp.float32)


def scores_of(q, k):
    return lax.dot_general(q, k, (((1,), (1,)), ((), ())), preferred_element_type=jnp.float32)


LOG2E = 1.4426950408889634
VMEM = pl.BlockSpec(memory_space=pltpu.VMEM)
SMEM = pl.BlockSpec(memory_space=pltpu.SMEM)
HBM = pl.BlockSpec(memory_space=pltpu.HBM)


def call(
    body, in_specs, out_shape, operands, flops, scratch=(), aliases=None, out_specs=None, mib=2
):
    spaces = {id(VMEM): pltpu.VMEM, id(HBM): pltpu.HBM}
    operands = [
        pltpu.with_memory_space_constraint(x, spaces[id(spec)]) if id(spec) in spaces else x
        for spec, x in zip(in_specs, operands)
    ]
    return pl.pallas_call(
        body,
        in_specs=in_specs,
        out_specs=out_specs if out_specs is not None else jax.tree.map(lambda _: VMEM, out_shape),
        out_shape=out_shape,
        scratch_shapes=list(scratch),
        input_output_aliases=aliases or {},
        compiler_params=pltpu.CompilerParams(vmem_limit_bytes=mib << 20),
        cost_estimate=pl.CostEstimate(flops=flops, bytes_accessed=1 << 20, transcendentals=0),
    )(*operands)


def load_piece(user, place, output_weight, piece_width):
    depth = output_weight.shape[0]

    def body(user_ref, place_ref, w_hbm, o_ref, sem):
        at = pl.ds(pl.multiple_of(user_ref[0] * piece_width, piece_width), piece_width)
        copy = pltpu.make_async_copy(w_hbm.at[:, at], o_ref, sem)
        copy.start()
        copy.wait()

    return call(
        body, [SMEM, SMEM, HBM], pltpu.VMEM((depth, piece_width), jnp.bfloat16),
        (user, place, output_weight), 0, [pltpu.SemaphoreType.DMA(())],
    )


def load_rows(sessions, boxes):
    n = len(boxes)

    def body(x_hbm, *refs):
        outs, sem = refs[:-1], refs[-1]
        copies = []
        for i, (r, rows, c, columns) in enumerate(boxes):
            src = x_hbm.at[pl.ds(r, rows), pl.ds(c, columns)]
            copies.append(pltpu.make_async_copy(src, outs[i], sem.at[i]))
        for copy in copies:
            copy.start()
        for copy in copies:
            copy.wait()

    return call(
        body, [HBM],
        [pltpu.VMEM((rows, columns), jnp.bfloat16) for _, rows, _, columns in boxes],
        (sessions,), 0, [pltpu.SemaphoreType.DMA((n,))],
    )


def project(parts, weight, kind, held, ahead):
    rows = parts[0].shape[0]
    _, depth, width = weight.shape
    wide = min(512, width)
    n = width // wide
    fetched = ([] if held is not None else [kind]) + ([] if ahead is None else [ahead])

    def body(*refs):
        x_refs, w_hbm = refs[:len(parts)], refs[len(parts)]
        bufs = refs[-1 - len(fetched):-1] if fetched else ()
        sem = refs[-1]
        o_ref = refs[len(parts) + 1 + (held is not None)]
        w_ref = refs[len(parts) + 1] if held is not None else bufs[0]

        def load(i, s):
            src = w_hbm.at[fetched[i], :, pl.ds(s * wide, wide)]
            return pltpu.make_async_copy(src, bufs[i].at[s], sem.at[i, s])

        for i in range(len(fetched)):
            for s in range(n):
                load(i, s).start()

        @pl.loop(0, n)
        def _(s):
            if held is None:
                pltpu.make_async_copy(w_hbm.at[0, :, pl.ds(0, wide)], w_ref.at[s], sem.at[0, s]).wait()
            at, total = 0, None
            for x_ref in x_refs:
                d = x_ref.shape[1]
                term = dot32(x_ref[...], w_ref[s, at:at + d, :])
                total = term if total is None else total + term
                at += d
            cols = pl.ds(pl.multiple_of(s * wide, wide), wide)
            o_ref[0, :, cols] = total.astype(jnp.bfloat16)

        if ahead is not None:
            for s in range(n):
                load(len(fetched) - 1, s).wait()

    operands = (*parts, weight) + (() if held is None else (held,))
    result, *weights = call(
        body, [VMEM] * len(parts) + [HBM] + [VMEM] * (held is not None),
        [pltpu.VMEM((1, rows, width), jnp.bfloat16)]
        + [pltpu.VMEM((n, depth, wide), jnp.bfloat16)] * len(fetched),
        operands, 2 * rows * depth * width,
        [pltpu.SemaphoreType.DMA((max(1, len(fetched)), n))],
    )
    return result, weights


def project_part(x, weights, offset, total, fetched):
    rows, depth = x.shape
    blocks = sum(w.shape[0] for w in weights)
    wide = weights[0].shape[2]
    across = blocks // 3

    def body(x_ref, *refs):
        w_refs, o_ref = refs[:len(weights)], refs[n_in - 1]
        base = 0

        def load(s):
            src = refs[n_in - 2].at[:, pl.ds(s * step, step)]
            return pltpu.make_async_copy(src, refs[n_in].at[s], refs[-1].at[s])

        if fetched is not None:
            for s in range(n_blocks):
                load(s).start()
        for w_ref in w_refs:
            n = w_ref.shape[0]

            @pl.loop(0, n)
            def _(s, w_ref=w_ref, base=base):
                t = s + base
                at = pl.ds(pl.multiple_of(lax.rem(t, across) * wide, wide), wide)
                part = dot32(x_ref[...], w_ref[s, offset:offset + depth, :])
                if total is not None:
                    part = refs[len(weights)][t // across, :, at] + part
                o_ref[t // across, :, at] = part

            base += n

        if fetched is not None:
            for s in range(n_blocks):
                load(s).wait()

    operands = (x, *weights) + (() if total is None else (total,))
    specs = [VMEM] * len(operands)
    aliases = {} if total is None else {len(operands) - 1: 0}
    shapes, scratch = [pltpu.VMEM((3, rows, across * wide), jnp.float32)], []
    if fetched is not None:
        step = min(512, fetched.shape[1])
        n_blocks = fetched.shape[1] // step
        operands += (fetched,)
        specs.append(HBM)
        shapes.append(pltpu.VMEM((n_blocks, fetched.shape[0], step), jnp.bfloat16))
        scratch.append(pltpu.SemaphoreType.DMA((n_blocks,)))
    n_in = len(operands)
    return call(
        body, specs, shapes, operands, 2 * rows * depth * blocks * wide, scratch,
        aliases=aliases,
    )


def biases(place, counts, rows):
    def body(place_ref, counts_ref, o_ref):
        mine = place_ref[0] * rows
        other = (1 - place_ref[0]) * rows
        for n, (query, key) in enumerate(((mine, mine), (mine, other), (other, mine), (other, other))):
            i = query + lax.broadcasted_iota(jnp.int32, (rows, 1), 0)
            first = jnp.zeros((rows, 1), jnp.int32)
            end = jnp.int32(0)
            for u in range(counts_ref.shape[0]):
                end = end + counts_ref[u]
                first = jnp.where(i >= end, end, first)
            j = key + lax.broadcasted_iota(jnp.int32, (rows, rows), 1)
            allowed = jnp.logical_and(j <= i, j >= first)
            o_ref[n] = jnp.where(allowed, 0.0, -1e30)

    return call(body, [SMEM, SMEM], pltpu.VMEM((4, rows, rows), jnp.float32), (place, counts), 0)


def softmax_parts(q, keys, values, masks):
    scores = [scores_of(q, k) * (HD ** (-0.5) * LOG2E) + b for k, b in zip(keys, masks)]
    top = functools.reduce(jnp.maximum, [jnp.max(s, axis=1, keepdims=True) for s in scores])
    raised = [jnp.exp2(s - top) for s in scores]
    total = sum(jnp.sum(p, axis=1, keepdims=True) for p in raised)
    out = sum(dot32(p.astype(jnp.bfloat16), v) for p, v in zip(raised, values))
    return top, total, out


def head_out(q, keys, values, masks):
    _, total, out = softmax_parts(q, keys, values, masks)
    return (out / total).astype(jnp.bfloat16)


def finish(place, x, weights, offset, total, own_k, own_v, bias, kv, r, splits):
    part_rows, depth = x.shape
    _, rows, width = total.shape
    wide = weights[0].shape[2]
    across = width // wide
    here = slice(r * part_rows, (r + 1) * part_rows)
    known = slice(0, (r + 1) * part_rows)

    def body(place_ref, x_ref, *refs):
        w_refs = refs[:len(weights)]
        t_ref, k_ref, v_ref, bias_ref = refs[len(weights):len(weights) + 4]
        mixed_refs, kv_ref, q_ref = refs[-2 - splits:-2], refs[-2], refs[-1]

        for c, w_ref in enumerate(w_refs):
            for g in range(across):
                cols = slice(g * wide, (g + 1) * wide)
                part = dot32(x_ref[...], w_ref[g, offset:offset + depth, :])
                part = (t_ref[c, here, cols] + part).astype(jnp.bfloat16)
                if c == 0:
                    q_ref[:, cols] = part
                else:
                    kv_ref[c - 1, here, cols] = part

        def heads(with_own):
            for h in range(width // HD):
                at = slice(h * HD, (h + 1) * HD)
                keys, values = [kv_ref[0, known, at]], [kv_ref[1, known, at]]
                masks = [bias_ref[3, here, known]]
                if with_own:
                    keys.append(k_ref[0, :, at])
                    values.append(v_ref[0, :, at])
                    masks.append(bias_ref[2, here, :])
                where = slice(h * HD % piece, h * HD % piece + HD)
                mixed_refs[h * HD // piece][:, where] = head_out(q_ref[:, at], keys, values, masks)

        pl.when(place_ref[0] == 0)(lambda: heads(True))
        pl.when(place_ref[0] != 0)(lambda: heads(False))

    piece = width // splits
    operands = (place, x, *weights, total, own_k, own_v, bias)
    aliases = {}
    if kv is not None:
        aliases = {len(operands): splits}
        operands += (kv,)
    specs = [SMEM] + [VMEM] * (len(operands) - 1)
    shapes = [pltpu.VMEM((part_rows, piece), jnp.bfloat16)] * splits
    shapes.append(pltpu.VMEM((2, rows, width), jnp.bfloat16))
    return call(
        body, specs, shapes, operands,
        6 * part_rows * depth * width + 8 * part_rows * rows * width,
        [pltpu.VMEM((part_rows, width), jnp.bfloat16)],
        aliases=aliases,
    )


def own_start(own_q, own_k, own_v, bias):
    _, rows, width = own_q.shape

    def body(q_ref, k_ref, v_ref, bias_ref, o_ref):
        for h in range(width // HD):
            at = slice(h * HD, (h + 1) * HD)
            o_ref[:, at] = head_out(
                q_ref[0, :, at], [k_ref[0, :, at]], [v_ref[0, :, at]], [bias_ref[0]]
            )

    return call(
        body, [VMEM] * 4, pltpu.VMEM((rows, width), jnp.bfloat16),
        (own_q, own_k, own_v, bias), 4 * rows * rows * width,
    )


def rest_heads(place_ref, q_ref, k_ref, v_ref, alone_ref, kv_ref, bias_ref, out_ref, heads):
    first = heads[0] * HD
    there = slice(first, (heads[-1] + 1) * HD)

    @pl.when(place_ref[0] == 0)
    def _():
        out_ref[...] = alone_ref[:, there]

    @pl.when(place_ref[0] != 0)
    def _():
        for h in heads:
            at = slice(h * HD, (h + 1) * HD)
            out_ref[:, h * HD - first:(h + 1) * HD - first] = head_out(
                q_ref[0, :, at], (k_ref[0, :, at], kv_ref[0, :, at]),
                (v_ref[0, :, at], kv_ref[1, :, at]), (bias_ref[0], bias_ref[1]),
            )


def own_rest(place, own_q, own_k, own_v, alone, kv, bias):
    _, rows, width = own_q.shape
    heads = range(width // HD // 2)

    def body(*refs):
        rest_heads(*refs, heads)

    return call(
        body, [SMEM] + [VMEM] * 6, pltpu.VMEM((rows, width // 2), jnp.bfloat16),
        (place, own_q, own_k, own_v, alone, kv, bias), 2 * rows * rows * width, mib=4,
    )


def own_out(place, own_q, own_k, own_v, alone, kv, bias, half, weight):
    rows, depth = alone.shape
    n, _, step = weight.shape
    heads = range(depth // HD // 2, depth // HD)
    cut = depth // 2

    def body(*refs):
        half_ref, w_ref, o_ref, rest = refs[7:]
        rest_heads(*refs[:7], rest, heads)

        @pl.loop(0, n)
        def _(s):
            part = dot32(half_ref[...], w_ref[s, :cut, :]) + dot32(rest[...], w_ref[s, cut:, :])
            o_ref[:, pl.ds(pl.multiple_of(s * step, step), step)] = part

    return call(
        body, [SMEM] + [VMEM] * 8, pltpu.VMEM((rows, n * step), jnp.float32),
        (place, own_q, own_k, own_v, alone, kv, bias, half, weight), 2 * rows * depth * n * step,
        [pltpu.VMEM((rows, depth // 2), jnp.bfloat16)],
        mib=5,
    )


def other_out(user, table, mixed, first, pieces, total, r, out, last):
    part_rows, depth = mixed.shape
    rows, model = total.shape
    wide = pieces[0].shape[-1]
    n = len(pieces)
    here = slice(r * part_rows, (r + 1) * part_rows)

    def body(user_ref, table_ref, mixed_ref, total_ref, *refs):
        piece_refs = refs[:n]

        def columns(s):
            return pl.ds(pl.multiple_of(table_ref[user_ref[0] * n + s] * wide, wide), wide)

        def store(s):
            o_ref, buf, sem = refs[-3:]
            dst = o_ref.at[pl.ds(r * part_rows, part_rows), columns(s)]
            return pltpu.make_async_copy(buf.at[s], dst, sem.at[s])

        for s in range(n):
            part = dot32(mixed_ref[...], piece_refs[s][first:first + depth, :])
            part = total_ref[here, columns(s)] + part
            if last:
                refs[-2][s] = part.astype(jnp.bfloat16)
                store(s).start()
            else:
                refs[-1][here, columns(s)] = part
        if last:
            for s in range(n):
                store(s).wait()

    operands = (user, table, mixed, total, *pieces) + (() if out is None else (out,))
    if last:
        aliases = {} if out is None else {len(operands) - 1: 0}
    else:
        aliases = {3: 0}
    return call(
        body,
        [SMEM, SMEM] + [VMEM] * (2 + n) + [HBM] * (out is not None),
        jax.ShapeDtypeStruct((rows, model), jnp.bfloat16) if last
        else pltpu.VMEM((rows, model), jnp.float32),
        operands, 2 * part_rows * depth * model,
        [pltpu.VMEM((n, part_rows, wide), jnp.bfloat16), pltpu.SemaphoreType.DMA((n,))] if last else (),
        aliases=aliases,
        out_specs=HBM if last else VMEM,
    )


def two_halves(ring, sessions, input_weight, output_weight, session_counts):
    users = 2 * len(ring)
    chips = len(ring)
    rows, model = sessions.shape
    place = lax.axis_index("heads").astype(jnp.int32)[None]
    user = lax.axis_index("users").astype(jnp.int32)[None]

    across = [(0, 1), (1, 0)]
    beside = [(a, b) for pair in ring for a, b in (pair, pair[::-1])]
    around = []
    for i in range(chips):
        around.append((ring[i][0], ring[(i + 1) % chips][0]))
        around.append((ring[i][1], ring[(i - 1) % chips][1]))

    full = (chips - 1) // 2
    half = chips % 2 == 0
    table = np.zeros((users, users), np.int32)
    for i in range(chips):
        for core in range(2):
            held = [(i, core), (i, 1 - core)]
            for k in range(1, full + 1):
                for c in (core, 1 - core):
                    source = (i - k) % chips if c == 0 else (i + k) % chips
                    held += [(source, c), (source, 1 - c)]
            if half:
                far = (i + chips // 2) % chips
                held += [(far, core), (far, 1 - core)]
            table[ring[i][core]] = [ring[a][b] for a, b in held]
    table = jnp.asarray(table.reshape(-1))

    sizes = [model // 2, model // 4, model // 4]
    offsets = np.cumsum([0] + sizes)[:-1].tolist()
    block = rows // 2
    piece = load_piece(user, place, output_weight, model // users)
    boxes = [(0, rows, o, s) for o, s in zip(offsets, sizes)]
    boxes += [(r * block, block, offsets[-1], sizes[-1]) for r in range(2)]
    loaded = load_rows(sessions, boxes)
    parts, sent = loaded[:3], [*loaded[:2], *loaded[3:]]

    crossed = lax.ppermute(piece, "heads", across)
    guests = [lax.ppermute(x, "heads", across) for x in sent]

    near, far = crossed, lax.ppermute(crossed, "users", beside)
    pieces = [near, far]
    for _ in range(full):
        near = lax.ppermute(near, "users", around)
        far = lax.ppermute(far, "users", around)
        pieces += [near, far]
        pieces += [lax.ppermute(near, "users", beside), lax.ppermute(far, "users", beside)]
    if half:
        near = lax.ppermute(near, "users", around)
        pieces += [near, lax.ppermute(near, "users", beside)]

    own_q, (w_q, w_k) = project(parts, input_weight, 0, None, 1)
    own_k, (w_v,) = project(parts, input_weight, 1, w_k, 2)
    own_v, _ = project(parts, input_weight, 2, w_v, None)
    weights = (w_q, w_k, w_v)
    bias = biases(place, session_counts, rows)
    total, = project_part(guests[0], weights, offsets[0], None, None)
    total, own_weight = project_part(guests[1], weights, offsets[1], total, output_weight)
    alone = own_start(own_q, own_k, own_v, bias)
    first, kv = finish(
        place, guests[2], weights, offsets[-1], total, own_k, own_v, bias, None, 0, 1
    )
    first = lax.ppermute(first, "heads", across)
    second, kv = finish(place, guests[3], weights, offsets[-1], total, own_k, own_v, bias, kv, 1, 1)
    second = lax.ppermute(second, "heads", across)
    half_mixed = own_rest(place, own_q, own_k, own_v, alone, kv, bias)
    total = own_out(place, own_q, own_k, own_v, alone, kv, bias, half_mixed, own_weight)
    out = other_out(user, table, first, 0, pieces, total, 0, None, True)
    return other_out(user, table, second, 0, pieces, total, 1, out, True)


def solution(mesh):
    in_specs = (P(("users", "heads"), None), P(None, None, "heads"), P("heads", None), P("users"))
    out_specs = P(("users", "heads"), None)
    if mesh.shape["heads"] == 2 and mesh.shape["users"] % 2 == 0 and mesh.shape["users"] > 2:
        per_device = functools.partial(two_halves, chip_ring(mesh))

        def layer(*args):
            return per_device(*args)

        return jax.shard_map(
            layer, mesh=mesh, in_specs=in_specs, out_specs=out_specs, check_vma=False
        )
    return jax.shard_map(
        gather_and_scatter, mesh=mesh, in_specs=in_specs, out_specs=out_specs, check_vma=False
    )
```

```python
import functools
import jax
import jax.numpy as jnp
import numpy as np
from jax import lax
from jax.experimental import pallas as pl
from jax.experimental.pallas import tpu as pltpu
from jax.sharding import PartitionSpec as P


HD = 128


def permitted(total, counts):
    positions = jnp.arange(total, dtype=jnp.int32)
    ends = jnp.cumsum(counts)
    row_user = jnp.sum((positions[:, None] >= ends[None, :]).astype(jnp.int32), axis=1)
    same_user = row_user[:, None] == row_user[None, :]
    return jnp.logical_and(same_user, positions[:, None] >= positions[None, :])


def attend(packed, allowed):
    total = packed.shape[1]
    width = packed.shape[2]
    block = min(512, total)
    count = total // block
    queries = packed[0].reshape(count, block, width // HD, HD)
    key_rows = packed[1].reshape(total, width // HD, HD)
    values = packed[2].reshape(total, width // HD, HD)
    masks = allowed.reshape(count, block, total)

    def one_block(pair):
        query_block, mask_block = pair
        scores = jnp.einsum(
            "qhe,khe->hqk", query_block, key_rows, preferred_element_type=jnp.float32
        ) * HD ** (-0.5)
        scores = jnp.where(mask_block[None], scores, -1e30)
        highest = jnp.max(scores, axis=2, keepdims=True)
        raised = jnp.where(mask_block[None], jnp.exp(scores - highest), 0.0)
        attn_probs = (raised / jnp.sum(raised, axis=2, keepdims=True)).astype(jnp.bfloat16)
        mixed = jnp.einsum("hqk,khe->qhe", attn_probs, values, preferred_element_type=jnp.float32)
        return mixed.astype(jnp.bfloat16).reshape(block, width)

    blocks_out = lax.map(one_block, (queries, masks))
    return blocks_out.reshape(total, width)


def gather_and_scatter(sessions, input_weight, output_weight, session_counts):
    packed = jnp.einsum(
        "nd,cde->cne",
        lax.all_gather(sessions, "heads", axis=0, tiled=True),
        input_weight,
        preferred_element_type=jnp.float32,
    ).astype(jnp.bfloat16)
    total = packed.shape[1]
    allowed = permitted(total, session_counts)
    mixed = attend(packed, allowed)
    return lax.psum_scatter(
        jnp.dot(mixed, output_weight, preferred_element_type=jnp.float32).astype(jnp.bfloat16),
        "heads",
        scatter_dimension=0,
        tiled=True,
    )


def chip_ring(mesh):
    column = mesh.devices.reshape(mesh.shape["users"], -1)[:, 0]
    by_chip = {}
    for user, device in enumerate(column):
        key = getattr(device, "coords", None)
        key = (user // 2,) if key is None else tuple(key)
        by_chip.setdefault(key, []).append(user)
    if any(len(users) != 2 for users in by_chip.values()):
        by_chip = {(i,): [2 * i, 2 * i + 1] for i in range(len(column) // 2)}
    keys = list(by_chip)

    def near(a, b):
        return sum(abs(i - j) for i, j in zip(a, b)) == 1

    budget = [20000]

    def extend(path, left):
        budget[0] -= 1
        if budget[0] < 0:
            return None
        if not left:
            return path if near(path[-1], path[0]) else None
        for key in sorted(k for k in left if near(k, path[-1])):
            found = extend(path + [key], left - {key})
            if found:
                return found
        return None

    order = extend([keys[0]], frozenset(keys[1:])) or keys
    return [tuple(by_chip[key]) for key in order]


def dot32(a, b):
    return jnp.dot(a, b, preferred_element_type=jnp.float32)


def scores_of(q, k):
    return lax.dot_general(q, k, (((1,), (1,)), ((), ())), preferred_element_type=jnp.float32)


LOG2E = 1.4426950408889634
VMEM = pl.BlockSpec(memory_space=pltpu.VMEM)
SMEM = pl.BlockSpec(memory_space=pltpu.SMEM)
HBM = pl.BlockSpec(memory_space=pltpu.HBM)


def call(
    body, in_specs, out_shape, operands, flops, scratch=(), aliases=None, out_specs=None, mib=2
):
    spaces = {id(VMEM): pltpu.VMEM, id(HBM): pltpu.HBM}
    operands = [
        pltpu.with_memory_space_constraint(x, spaces[id(spec)]) if id(spec) in spaces else x
        for spec, x in zip(in_specs, operands)
    ]
    return pl.pallas_call(
        body,
        in_specs=in_specs,
        out_specs=out_specs if out_specs is not None else jax.tree.map(lambda _: VMEM, out_shape),
        out_shape=out_shape,
        scratch_shapes=list(scratch),
        input_output_aliases=aliases or {},
        compiler_params=pltpu.CompilerParams(vmem_limit_bytes=mib << 20),
        cost_estimate=pl.CostEstimate(flops=flops, bytes_accessed=1 << 20, transcendentals=0),
    )(*operands)


def load_piece(user, place, output_weight, piece_width):
    depth = output_weight.shape[0]

    def body(user_ref, place_ref, w_hbm, o_ref, sem):
        at = pl.ds(pl.multiple_of(user_ref[0] * piece_width, piece_width), piece_width)
        copy = pltpu.make_async_copy(w_hbm.at[:, at], o_ref, sem)
        copy.start()
        copy.wait()

    return call(
        body, [SMEM, SMEM, HBM], pltpu.VMEM((depth, piece_width), jnp.bfloat16),
        (user, place, output_weight), 0, [pltpu.SemaphoreType.DMA(())],
    )


def load_rows(sessions, boxes):
    n = len(boxes)

    def body(x_hbm, *refs):
        outs, sem = refs[:-1], refs[-1]
        copies = []
        for i, (r, rows, c, columns) in enumerate(boxes):
            src = x_hbm.at[pl.ds(r, rows), pl.ds(c, columns)]
            copies.append(pltpu.make_async_copy(src, outs[i], sem.at[i]))
        for copy in copies:
            copy.start()
        for copy in copies:
            copy.wait()

    return call(
        body, [HBM],
        [pltpu.VMEM((rows, columns), jnp.bfloat16) for _, rows, _, columns in boxes],
        (sessions,), 0, [pltpu.SemaphoreType.DMA((n,))],
    )


def project(parts, weight, kind, held, ahead):
    rows = parts[0].shape[0]
    _, depth, width = weight.shape
    wide = min(512, width)
    n = width // wide
    fetched = ([] if held is not None else [kind]) + ([] if ahead is None else [ahead])

    def body(*refs):
        x_refs, w_hbm = refs[:len(parts)], refs[len(parts)]
        bufs = refs[-1 - len(fetched):-1] if fetched else ()
        sem = refs[-1]
        o_ref = refs[len(parts) + 1 + (held is not None)]
        w_ref = refs[len(parts) + 1] if held is not None else bufs[0]

        def load(i, s):
            src = w_hbm.at[fetched[i], :, pl.ds(s * wide, wide)]
            return pltpu.make_async_copy(src, bufs[i].at[s], sem.at[i, s])

        for i in range(len(fetched)):
            for s in range(n):
                load(i, s).start()

        @pl.loop(0, n)
        def _(s):
            if held is None:
                pltpu.make_async_copy(w_hbm.at[0, :, pl.ds(0, wide)], w_ref.at[s], sem.at[0, s]).wait()
            at, total = 0, None
            for x_ref in x_refs:
                d = x_ref.shape[1]
                term = dot32(x_ref[...], w_ref[s, at:at + d, :])
                total = term if total is None else total + term
                at += d
            cols = pl.ds(pl.multiple_of(s * wide, wide), wide)
            o_ref[0, :, cols] = total.astype(jnp.bfloat16)

        if ahead is not None:
            for s in range(n):
                load(len(fetched) - 1, s).wait()

    operands = (*parts, weight) + (() if held is None else (held,))
    result, *weights = call(
        body, [VMEM] * len(parts) + [HBM] + [VMEM] * (held is not None),
        [pltpu.VMEM((1, rows, width), jnp.bfloat16)]
        + [pltpu.VMEM((n, depth, wide), jnp.bfloat16)] * len(fetched),
        operands, 2 * rows * depth * width,
        [pltpu.SemaphoreType.DMA((max(1, len(fetched)), n))],
    )
    return result, weights


def project_part(x, weights, offset, total, fetched):
    rows, depth = x.shape
    blocks = sum(w.shape[0] for w in weights)
    wide = weights[0].shape[2]
    across = blocks // 3

    def body(x_ref, *refs):
        w_refs, o_ref = refs[:len(weights)], refs[n_in - 1]
        base = 0

        def load(s):
            src = refs[n_in - 2].at[:, pl.ds(s * step, step)]
            return pltpu.make_async_copy(src, refs[n_in].at[s], refs[-1].at[s])

        if fetched is not None:
            for s in range(n_blocks):
                load(s).start()
        for w_ref in w_refs:
            n = w_ref.shape[0]

            @pl.loop(0, n)
            def _(s, w_ref=w_ref, base=base):
                t = s + base
                at = pl.ds(pl.multiple_of(lax.rem(t, across) * wide, wide), wide)
                part = dot32(x_ref[...], w_ref[s, offset:offset + depth, :])
                if total is not None:
                    part = refs[len(weights)][t // across, :, at] + part
                o_ref[t // across, :, at] = part

            base += n

        if fetched is not None:
            for s in range(n_blocks):
                load(s).wait()

    operands = (x, *weights) + (() if total is None else (total,))
    specs = [VMEM] * len(operands)
    aliases = {} if total is None else {len(operands) - 1: 0}
    shapes, scratch = [pltpu.VMEM((3, rows, across * wide), jnp.float32)], []
    if fetched is not None:
        step = min(512, fetched.shape[1])
        n_blocks = fetched.shape[1] // step
        operands += (fetched,)
        specs.append(HBM)
        shapes.append(pltpu.VMEM((n_blocks, fetched.shape[0], step), jnp.bfloat16))
        scratch.append(pltpu.SemaphoreType.DMA((n_blocks,)))
    n_in = len(operands)
    return call(
        body, specs, shapes, operands, 2 * rows * depth * blocks * wide, scratch,
        aliases=aliases,
    )


def biases(place, counts, rows):
    def body(place_ref, counts_ref, o_ref):
        mine = place_ref[0] * rows
        other = (1 - place_ref[0]) * rows
        for n, (query, key) in enumerate(((mine, mine), (mine, other), (other, mine), (other, other))):
            i = query + lax.broadcasted_iota(jnp.int32, (rows, 1), 0)
            first = jnp.zeros((rows, 1), jnp.int32)
            end = jnp.int32(0)
            for u in range(counts_ref.shape[0]):
                end = end + counts_ref[u]
                first = jnp.where(i >= end, end, first)
            j = key + lax.broadcasted_iota(jnp.int32, (rows, rows), 1)
            allowed = jnp.logical_and(j <= i, j >= first)
            o_ref[n] = jnp.where(allowed, 0.0, -1e30)

    return call(body, [SMEM, SMEM], pltpu.VMEM((4, rows, rows), jnp.float32), (place, counts), 0)


def softmax_parts(q, keys, values, masks):
    scores = [scores_of(q, k) * (HD ** (-0.5) * LOG2E) + b for k, b in zip(keys, masks)]
    top = functools.reduce(jnp.maximum, [jnp.max(s, axis=1, keepdims=True) for s in scores])
    raised = [jnp.exp2(s - top) for s in scores]
    total = sum(jnp.sum(p, axis=1, keepdims=True) for p in raised)
    out = sum(dot32(p.astype(jnp.bfloat16), v) for p, v in zip(raised, values))
    return top, total, out


def head_out(q, keys, values, masks):
    _, total, out = softmax_parts(q, keys, values, masks)
    return (out / total).astype(jnp.bfloat16)


def finish(place, x, weights, offset, total, own_k, own_v, bias, kv, row, splits):
    part_rows, depth = x.shape
    _, rows, width = total.shape
    wide = weights[0].shape[2]
    across = width // wide
    here = slice(row, row + part_rows)
    known = slice(0, row + part_rows)

    def body(place_ref, x_ref, *refs):
        w_refs = refs[:len(weights)]
        t_ref, k_ref, v_ref, bias_ref = refs[len(weights):len(weights) + 4]
        mixed_refs, kv_ref, q_ref = refs[-2 - splits:-2], refs[-2], refs[-1]

        for c, w_ref in enumerate(w_refs):
            for g in range(across):
                cols = slice(g * wide, (g + 1) * wide)
                part = dot32(x_ref[...], w_ref[g, offset:offset + depth, :])
                part = (t_ref[c, here, cols] + part).astype(jnp.bfloat16)
                if c == 0:
                    q_ref[:, cols] = part
                else:
                    kv_ref[c - 1, here, cols] = part

        def heads(with_own):
            for h in range(width // HD):
                at = slice(h * HD, (h + 1) * HD)
                keys, values = [kv_ref[0, known, at]], [kv_ref[1, known, at]]
                masks = [bias_ref[3, here, known]]
                if with_own:
                    keys.append(k_ref[0, :, at])
                    values.append(v_ref[0, :, at])
                    masks.append(bias_ref[2, here, :])
                where = slice(h * HD % piece, h * HD % piece + HD)
                mixed_refs[h * HD // piece][:, where] = head_out(q_ref[:, at], keys, values, masks)

        pl.when(place_ref[0] == 0)(lambda: heads(True))
        pl.when(place_ref[0] != 0)(lambda: heads(False))

    piece = width // splits
    operands = (place, x, *weights, total, own_k, own_v, bias)
    aliases = {}
    if kv is not None:
        aliases = {len(operands): splits}
        operands += (kv,)
    specs = [SMEM] + [VMEM] * (len(operands) - 1)
    shapes = [pltpu.VMEM((part_rows, piece), jnp.bfloat16)] * splits
    shapes.append(pltpu.VMEM((2, rows, width), jnp.bfloat16))
    return call(
        body, specs, shapes, operands,
        6 * part_rows * depth * width + 8 * part_rows * rows * width,
        [pltpu.VMEM((part_rows, width), jnp.bfloat16)],
        aliases=aliases,
    )


def own_start(own_q, own_k, own_v, bias):
    _, rows, width = own_q.shape

    def body(q_ref, k_ref, v_ref, bias_ref, o_ref):
        for h in range(width // HD):
            at = slice(h * HD, (h + 1) * HD)
            o_ref[:, at] = head_out(
                q_ref[0, :, at], [k_ref[0, :, at]], [v_ref[0, :, at]], [bias_ref[0]]
            )

    return call(
        body, [VMEM] * 4, pltpu.VMEM((rows, width), jnp.bfloat16),
        (own_q, own_k, own_v, bias), 4 * rows * rows * width,
    )


def rest_heads(place_ref, q_ref, k_ref, v_ref, alone_ref, kv_ref, bias_ref, out_ref, heads):
    first = heads[0] * HD
    there = slice(first, (heads[-1] + 1) * HD)

    @pl.when(place_ref[0] == 0)
    def _():
        out_ref[...] = alone_ref[:, there]

    @pl.when(place_ref[0] != 0)
    def _():
        for h in heads:
            at = slice(h * HD, (h + 1) * HD)
            out_ref[:, h * HD - first:(h + 1) * HD - first] = head_out(
                q_ref[0, :, at], (k_ref[0, :, at], kv_ref[0, :, at]),
                (v_ref[0, :, at], kv_ref[1, :, at]), (bias_ref[0], bias_ref[1]),
            )


def own_rest(place, own_q, own_k, own_v, alone, kv, bias):
    _, rows, width = own_q.shape
    heads = range(width // HD // 2)

    def body(*refs):
        rest_heads(*refs, heads)

    return call(
        body, [SMEM] + [VMEM] * 6, pltpu.VMEM((rows, width // 2), jnp.bfloat16),
        (place, own_q, own_k, own_v, alone, kv, bias), 2 * rows * rows * width, mib=4,
    )


def own_out(place, own_q, own_k, own_v, alone, kv, bias, half, weight):
    rows, depth = alone.shape
    n, _, step = weight.shape
    heads = range(depth // HD // 2, depth // HD)
    cut = depth // 2

    def body(*refs):
        half_ref, w_ref, o_ref, rest = refs[7:]
        rest_heads(*refs[:7], rest, heads)

        @pl.loop(0, n)
        def _(s):
            part = dot32(half_ref[...], w_ref[s, :cut, :]) + dot32(rest[...], w_ref[s, cut:, :])
            o_ref[:, pl.ds(pl.multiple_of(s * step, step), step)] = part

    return call(
        body, [SMEM] + [VMEM] * 8, pltpu.VMEM((rows, n * step), jnp.float32),
        (place, own_q, own_k, own_v, alone, kv, bias, half, weight), 2 * rows * depth * n * step,
        [pltpu.VMEM((rows, depth // 2), jnp.bfloat16)],
        mib=5,
    )


def other_out(user, table, mixed, first, pieces, total, row, out, last):
    part_rows, depth = mixed.shape
    rows, model = total.shape
    wide = pieces[0].shape[-1]
    n = len(pieces)
    here = slice(row, row + part_rows)

    def body(user_ref, table_ref, mixed_ref, total_ref, *refs):
        piece_refs = refs[:n]

        def columns(s):
            return pl.ds(pl.multiple_of(table_ref[user_ref[0] * n + s] * wide, wide), wide)

        def store(s):
            o_ref, buf, sem = refs[-3:]
            dst = o_ref.at[pl.ds(row, part_rows), columns(s)]
            return pltpu.make_async_copy(buf.at[s], dst, sem.at[s])

        for s in range(n):
            part = dot32(mixed_ref[...], piece_refs[s][first:first + depth, :])
            part = total_ref[here, columns(s)] + part
            if last:
                refs[-2][s] = part.astype(jnp.bfloat16)
                store(s).start()
            else:
                refs[-1][here, columns(s)] = part
        if last:
            for s in range(n):
                store(s).wait()

    operands = (user, table, mixed, total, *pieces) + (() if out is None else (out,))
    if last:
        aliases = {} if out is None else {len(operands) - 1: 0}
    else:
        aliases = {3: 0}
    return call(
        body,
        [SMEM, SMEM] + [VMEM] * (2 + n) + [HBM] * (out is not None),
        jax.ShapeDtypeStruct((rows, model), jnp.bfloat16) if last
        else pltpu.VMEM((rows, model), jnp.float32),
        operands, 2 * part_rows * depth * model,
        [pltpu.VMEM((n, part_rows, wide), jnp.bfloat16), pltpu.SemaphoreType.DMA((n,))] if last else (),
        aliases=aliases,
        out_specs=HBM if last else VMEM,
    )


def two_halves(ring, sessions, input_weight, output_weight, session_counts):
    users = 2 * len(ring)
    chips = len(ring)
    rows, model = sessions.shape
    place = lax.axis_index("heads").astype(jnp.int32)[None]
    user = lax.axis_index("users").astype(jnp.int32)[None]

    across = [(0, 1), (1, 0)]
    beside = [(a, b) for pair in ring for a, b in (pair, pair[::-1])]
    around = []
    for i in range(chips):
        around.append((ring[i][0], ring[(i + 1) % chips][0]))
        around.append((ring[i][1], ring[(i - 1) % chips][1]))

    full = (chips - 1) // 2
    half = chips % 2 == 0
    table = np.zeros((users, users), np.int32)
    for i in range(chips):
        for core in range(2):
            held = [(i, core), (i, 1 - core)]
            for k in range(1, full + 1):
                for c in (core, 1 - core):
                    source = (i - k) % chips if c == 0 else (i + k) % chips
                    held += [(source, c), (source, 1 - c)]
            if half:
                far = (i + chips // 2) % chips
                held += [(far, core), (far, 1 - core)]
            table[ring[i][core]] = [ring[a][b] for a, b in held]
    table = jnp.asarray(table.reshape(-1))

    sizes = [model // 2, model // 4, model // 4]
    offsets = np.cumsum([0] + sizes)[:-1].tolist()
    block = max(16, rows * 7 // 256 * 16)
    piece = load_piece(user, place, output_weight, model // users)
    boxes = [(0, rows, o, s) for o, s in zip(offsets, sizes)]
    boxes += [(r, n, offsets[-1], sizes[-1]) for r, n in ((0, block), (block, rows - block))]
    loaded = load_rows(sessions, boxes)
    parts, sent = loaded[:3], [*loaded[:2], *loaded[3:]]

    crossed = lax.ppermute(piece, "heads", across)
    guests = [lax.ppermute(x, "heads", across) for x in sent]

    near, far = crossed, lax.ppermute(crossed, "users", beside)
    pieces = [near, far]
    for _ in range(full):
        near = lax.ppermute(near, "users", around)
        far = lax.ppermute(far, "users", around)
        pieces += [near, far]
        pieces += [lax.ppermute(near, "users", beside), lax.ppermute(far, "users", beside)]
    if half:
        near = lax.ppermute(near, "users", around)
        pieces += [near, lax.ppermute(near, "users", beside)]

    own_q, (w_q, w_k) = project(parts, input_weight, 0, None, 1)
    own_k, (w_v,) = project(parts, input_weight, 1, w_k, 2)
    own_v, _ = project(parts, input_weight, 2, w_v, None)
    weights = (w_q, w_k, w_v)
    bias = biases(place, session_counts, rows)
    total, = project_part(guests[0], weights, offsets[0], None, None)
    total, own_weight = project_part(guests[1], weights, offsets[1], total, output_weight)
    alone = own_start(own_q, own_k, own_v, bias)
    first, kv = finish(
        place, guests[2], weights, offsets[-1], total, own_k, own_v, bias, None, 0, 1
    )
    first = lax.ppermute(first, "heads", across)
    second, kv = finish(
        place, guests[3], weights, offsets[-1], total, own_k, own_v, bias, kv, block, 1
    )
    second = lax.ppermute(second, "heads", across)
    half_mixed = own_rest(place, own_q, own_k, own_v, alone, kv, bias)
    total = own_out(place, own_q, own_k, own_v, alone, kv, bias, half_mixed, own_weight)
    out = other_out(user, table, first, 0, pieces, total, 0, None, True)
    return other_out(user, table, second, 0, pieces, total, block, out, True)


def solution(mesh):
    in_specs = (P(("users", "heads"), None), P(None, None, "heads"), P("heads", None), P("users"))
    out_specs = P(("users", "heads"), None)
    if mesh.shape["heads"] == 2 and mesh.shape["users"] % 2 == 0 and mesh.shape["users"] > 2:
        per_device = functools.partial(two_halves, chip_ring(mesh))

        def layer(*args):
            return per_device(*args)

        return jax.shard_map(
            layer, mesh=mesh, in_specs=in_specs, out_specs=out_specs, check_vma=False
        )
    return jax.shard_map(
        gather_and_scatter, mesh=mesh, in_specs=in_specs, out_specs=out_specs, check_vma=False
    )
```
